32 devices in a mesh: pipe: 4 (over y, x), ctx: 2 (over core), tp: 4 (over z).
Axes of the slice: x: 2, y: 2, z: 4, core: 2. Of those that a mesh axis runs over, the one named last changes fastest.
Arguments:
- mamba_input: bfloat16 [4, 768, 8192], P('pipe', 'ctx', 'tp'), may hold values from -6 to 6
- mamba_bc: bfloat16 [4, 768, 2, 512], P('pipe', 'ctx', None, 'tp'), may hold values from -6 to 6
- gate_input: bfloat16 [4, 768, 8192], P('pipe', 'ctx', 'tp'), may hold values from -6 to 6
- step_input: bfloat16 [4, 768, 128], P('pipe', 'ctx', 'tp'), may hold values from -4 to 4
- step_bias: float32 [4, 128], P('pipe', 'tp'), may hold values from -1 to 1
- decay_rate: float32 [4, 128], P('pipe', 'tp'), may hold values from 6.510417e-05 to 0.03
- skip_gain: float32 [4, 128], P('pipe', 'tp'), may hold values from 0.5 to 1.5
- conv_weight: float32 [4, 4, 8192], P('pipe', None, 'tp'), may hold values from -3 to 3
- conv_bc_weight: float32 [4, 4, 2, 512], P('pipe', None, None, 'tp'), may hold values from -3 to 3
- norm_gain: float32 [4, 8192], P('pipe', 'tp'), may hold values from 0.5 to 1.5
- queries: bfloat16 [4, 768, 4096], P('pipe', 'ctx', 'tp'), may hold values from -160 to 160
- attn_keys: bfloat16 [4, 768, 512], P('pipe', 'ctx', 'tp'), may hold values from -7 to 7
- attn_values: bfloat16 [4, 768, 512], P('pipe', 'ctx', 'tp'), may hold values from -6 to 6
- documents: int32 [4, 768], P('pipe'), may hold values from 0 to 3, never falling along the last dimension, each value on 1 to 384 neighbouring positions
Outputs:
- mixer_out: bfloat16 [4, 768, 8192], P('pipe', 'ctx', 'tp')
- attn_out: bfloat16 [4, 768, 4096], P('pipe', 'ctx', 'tp')
The draws below stay inside these ranges and needn't reach their ends.
All inputs are finite; a program needn't handle non-finite values.
Results may differ from the reference program's by a relative error of at most 0.0035.
Values may be sent and summed in bfloat16 or wider, within the bound.
A program may use at most 64 MiB of HBM per device.

```python
import math
import jax
import jax.numpy as jnp
import numpy as np
from jax import lax

HEADS = 128
HDIM = 64
STATE = 128
GROUPS = 4
KERNEL = 4
QHEADS = 32
KVHEADS = 4
ADIM = 128
DOCS = 4
TOK_DEV = 384
INNER = 8192
TOKENS = 768
SECTIONS = 4


def query_key_pair(key):
    key_seed = jax.random.fold_in(key, 101)
    query_seed = jax.random.fold_in(key, 102)
    keys_all = jnp.clip(jax.random.normal(key_seed, (SECTIONS, TOKENS, KVHEADS, ADIM), jnp.float32), -6.0, 6.0)
    queries_all = jnp.clip(jax.random.normal(query_seed, (SECTIONS, TOKENS, QHEADS, ADIM), jnp.float32), -6.0, 6.0)
    return (queries_all.reshape(SECTIONS, TOKENS, QHEADS * ADIM), keys_all.reshape(SECTIONS, TOKENS, KVHEADS * ADIM))


def draw_queries(key, part):
    return query_key_pair(key)[0].astype(jnp.bfloat16)


def draw_attn_keys(key, part):
    return query_key_pair(key)[1].astype(jnp.bfloat16)


def block_levels(stream_key, shape, cuts, least, largest):
    gain, own = 1.0, jax.random.fold_in(stream_key, 6)
    for dim, parts in cuts:
        heights = jnp.exp(jax.random.uniform(jax.random.fold_in(own, dim), (parts,), jnp.float32, least / len(cuts), largest / len(cuts)))
        gain = gain * jnp.repeat(heights, shape[dim] // parts).reshape([-1 if axis == dim else 1 for axis in range(len(shape))])
    return gain


def profile(number_of, total, reach, lean):
    loads = [(1 << 20) // math.isqrt(rank ** lean) + 1 for rank in range(2, number_of + 1)]
    spare, given = total - reach - (number_of - 1), [1] * (number_of - 1)
    while spare > 0:
        candidates = [i for i in range(number_of - 1) if given[i] < reach]
        pool, left = sum([loads[i] for i in candidates]), spare
        for i in candidates:
            addition = min(reach - given[i], max(1, left * loads[i] // pool), spare)
            given[i] = given[i] + addition
            spare = spare - addition
    return np.array([reach] + given)


def ragged_sizes(key, number_of, total, most, slope):
    if number_of == 2:
        one = jax.random.randint(key, (), max(1, total - most), min(most, total - 1) + 1)
        return jnp.stack([one, total - one])
    tallies = jnp.asarray(profile(number_of, total, most, slope), jnp.int32)
    couples = (number_of - 1) // 2
    source_of, receiver = tallies[1:1 + 2 * couples:2], tallies[2:2 + 2 * couples:2]
    room = jnp.minimum(source_of - 1, most - receiver)
    moved = jax.random.randint(jax.random.fold_in(key, 1), (couples,), 0, 1 << 20) % (room + 1)
    tallies = tallies.at[1:1 + 2 * couples:2].set(source_of - moved).at[2:2 + 2 * couples:2].set(receiver + moved)
    return tallies[jax.random.permutation(jax.random.fold_in(key, 2), number_of)]


def centred(rng, dims, deviation, bound, cuts=(), held_as=jnp.bfloat16):
    loudness = block_levels(rng, dims, cuts, -0.22, 0.18) if cuts else 1.0
    values = jax.random.normal(rng, dims, jnp.float32) * deviation * loudness
    return jnp.minimum(jnp.maximum(values, -bound), bound).astype(held_as)


def setup_inputs(seed: int = 0) -> dict:
    arg_keys = jax.random.split(jax.random.key(seed), 15)
    return {
        "mamba_input": centred(arg_keys[0], (SECTIONS, TOKENS, INNER), 1.0, 6.0, ((0, 4), (1, 2), (2, 4))),
        "mamba_bc": centred(arg_keys[1], (SECTIONS, TOKENS, 2, GROUPS * STATE), 1.0, 6.0, ((0, 4), (1, 2), (3, 4))),
        "gate_input": centred(arg_keys[2], (SECTIONS, TOKENS, INNER), 1.0, 6.0, ((0, 4), (1, 2), (2, 4))),
        "step_input": centred(arg_keys[3], (SECTIONS, TOKENS, HEADS), 1.0, 4.0, ((0, 4), (1, 2), (2, 4))),
        "step_bias": jnp.clip(jax.random.uniform(arg_keys[4], (SECTIONS, HEADS), jnp.float32, -1.0, 1.0) * block_levels(arg_keys[4], (SECTIONS, HEADS), ((0, 4), (1, 4)), -0.4, 0.0), -1.0, 1.0),
        "decay_rate": jnp.clip(jnp.exp(math.log(0.03) - 6.132964 * jax.random.uniform(arg_keys[5], (SECTIONS, HEADS), jnp.float32) ** block_levels(arg_keys[5], (SECTIONS, HEADS), ((0, 4), (1, 4)), -0.2, 0.2)), 6.510417006211355e-05, 0.03),
        "skip_gain": jnp.clip(0.5 + 1.0 * jax.random.uniform(arg_keys[6], (SECTIONS, HEADS), jnp.float32) ** block_levels(arg_keys[6], (SECTIONS, HEADS), ((0, 4), (1, 4)), -0.2, 0.2), 0.5, 1.5),
        "conv_weight": centred(arg_keys[7], (SECTIONS, KERNEL, INNER), KERNEL ** -0.5, 3.0, ((0, 4), (2, 4)), jnp.float32),
        "conv_bc_weight": centred(arg_keys[8], (SECTIONS, KERNEL, 2, GROUPS * STATE), KERNEL ** -0.5, 3.0, ((0, 4), (3, 4)), jnp.float32),
        "norm_gain": jnp.clip(1.0 + 0.1 * jax.random.normal(arg_keys[9], (SECTIONS, INNER), jnp.float32), 0.5, 1.5),
        "queries": draw_queries(jax.random.fold_in(arg_keys[14], 71), 0),
        "attn_keys": draw_attn_keys(jax.random.fold_in(arg_keys[14], 71), 0),
        "attn_values": centred(arg_keys[12], (SECTIONS, TOKENS, KVHEADS * ADIM), 1.0, 6.0, ((0, 4), (1, 2), (2, 4))),
        "documents": jax.vmap(lambda own: jnp.searchsorted(jnp.cumsum(ragged_sizes(own, DOCS, TOKENS, TOKENS // 2, 1)), jnp.arange(TOKENS), side="right"))(jax.random.split(arg_keys[13], SECTIONS)).reshape((SECTIONS, TOKENS)).astype(jnp.int32),
    }


highest = lax.Precision.HIGHEST

def conv_silu(padded, weight, length):
    summed = jnp.zeros((length,) + padded.shape[1:], jnp.float32)
    for offset in range(weight.shape[0]):
        summed = summed + weight[offset] * padded[offset:offset + length].astype(jnp.float32)
    return jax.nn.silu(summed)

def local_scan(x_block, b_block, c_block, step_block, log_block, groups):
    length, head_count, head_size = x_block.shape
    per_group = head_count // groups
    cumulative = jnp.cumsum(log_block, axis=0)
    gram_matrix = jnp.einsum('tgn,sgn->gts', c_block, b_block, precision=highest)
    spread = cumulative.T[:, :, None] - cumulative.T[:, None, :]
    row_index = lax.broadcasted_iota(jnp.int32, (length, length), 0)
    col_index = lax.broadcasted_iota(jnp.int32, (length, length), 1)
    decays = jnp.exp(jnp.where(row_index >= col_index, spread, -jnp.inf))
    weights = decays.reshape(groups, per_group, length, length) * gram_matrix[:, None] * step_block.T.reshape(groups, per_group, 1, length)
    inside = jnp.einsum('ghts,sghp->tghp', weights, x_block.reshape(length, groups, per_group, head_size), precision=highest)
    inside = inside.reshape(length, head_count, head_size)
    end_log = cumulative[-1]
    tail_decay = jnp.exp(end_log[None, :] - cumulative) * step_block
    weighted = (x_block * tail_decay[:, :, None]).reshape(length, groups, per_group, head_size)
    contrib = jnp.einsum('tgn,tghp->ghpn', b_block, weighted, precision=highest).reshape(head_count, head_size, -1)
    return (inside, contrib, jnp.exp(end_log), cumulative)

def incoming_term(c_block, carried, cumulative, groups):
    length, head_count = cumulative.shape
    head_size = carried.shape[1]
    per_group = head_count // groups
    grid = carried.reshape(groups, per_group, head_size, -1)
    result = jnp.einsum('tgn,ghpn->tghp', c_block, grid, precision=highest).reshape(length, head_count, head_size)
    return result * jnp.exp(cumulative)[:, :, None]

def gated_norm(ssd_out, gate_in, gain_in, groups):
    gated_out = ssd_out * jax.nn.silu(gate_in.astype(jnp.float32))
    row_count, width = gated_out.shape
    grouped = gated_out.reshape(row_count, groups, width // groups)
    mean_square = lax.optimization_barrier(jnp.mean(grouped * grouped, axis=-1, keepdims=True))
    normed = (grouped * lax.rsqrt(mean_square + 1e-05)).reshape(row_count, width)
    return (normed * gain_in).astype(jnp.bfloat16)

def mamba_section(mamba_input, mamba_bc, gate_input, step_input, step_bias, decay_rate, skip_gain, conv_weight, conv_bc_weight, norm_gain):
    margin = KERNEL - 1
    x_padded = jnp.concatenate([jnp.zeros((margin, INNER), mamba_input.dtype), mamba_input], 0)
    x_conv = conv_silu(x_padded, conv_weight, TOKENS)
    bc_padded = jnp.concatenate([jnp.zeros((margin, 2, GROUPS * STATE), mamba_bc.dtype), mamba_bc], 0)
    bc_conv = conv_silu(bc_padded, conv_bc_weight, TOKENS)
    step_size = jax.nn.softplus(step_input.astype(jnp.float32) + step_bias)
    log_decay = -decay_rate * step_size
    blocks = TOKENS // TOK_DEV
    x_blocks = x_conv.reshape(blocks, TOK_DEV, HEADS, HDIM)
    b_blocks = bc_conv[:, 0].reshape(blocks, TOK_DEV, GROUPS, STATE)
    c_blocks = bc_conv[:, 1].reshape(blocks, TOK_DEV, GROUPS, STATE)
    step_blocks = step_size.reshape(blocks, TOK_DEV, HEADS)
    log_blocks = log_decay.reshape(blocks, TOK_DEV, HEADS)

    def advance(carried, pieces):
        x_block, b_block, c_block, step_block, log_block = pieces
        inside, contrib, shard_decay, cumulative = local_scan(x_block, b_block, c_block, step_block, log_block, GROUPS)
        incoming_part = incoming_term(c_block, carried, cumulative, GROUPS)
        output = inside + incoming_part + skip_gain[None, :, None] * x_block
        return (shard_decay[:, None, None] * carried + contrib, output)
    initial = jnp.zeros((HEADS, HDIM, STATE), jnp.float32)
    unused, outputs = lax.scan(advance, initial, (x_blocks, b_blocks, c_blocks, step_blocks, log_blocks))
    ssd_out = outputs.reshape(TOKENS, INNER)
    return gated_norm(ssd_out, gate_input, norm_gain, GROUPS)

def attend_section(queries, attn_keys, attn_values, documents):
    per_kv = QHEADS // KVHEADS
    logit_scale = 1.0 / math.sqrt(ADIM)
    key_widened = attn_keys.astype(jnp.float32).reshape(TOKENS, KVHEADS, ADIM)
    value_widened = attn_values.astype(jnp.float32).reshape(TOKENS, KVHEADS, ADIM)
    positions = jnp.arange(TOKENS, dtype=jnp.int32)
    blocks = TOKENS // TOK_DEV
    query_blocks = queries.reshape(blocks, TOK_DEV, KVHEADS, per_kv, ADIM)

    def one_block(pieces):
        query_tile, first_row = pieces
        query_pos = first_row + jnp.arange(TOK_DEV, dtype=jnp.int32)
        query_doc = lax.dynamic_slice_in_dim(documents, first_row, TOK_DEV)
        attention_logits = jnp.einsum('hbau,zbu->bahz', query_tile.astype(jnp.float32), key_widened) * logit_scale
        allowed = (positions[None, :] <= query_pos[:, None]) & (documents[None, :] == query_doc[:, None])
        masked = jnp.where(allowed, attention_logits, -1e+30)
        row_max = lax.optimization_barrier(jnp.max(masked, axis=-1, keepdims=True))
        weights_exp = jnp.where(allowed, jnp.exp(masked - row_max), 0.0)
        row_sum_running = lax.optimization_barrier(jnp.sum(weights_exp, axis=-1))
        rounded_result = lax.optimization_barrier(weights_exp.astype(jnp.bfloat16)).astype(jnp.float32)
        mixer_result = jnp.einsum('ljnx,xlc->ljnc', rounded_result, value_widened) / row_sum_running[..., None]
        return mixer_result.transpose(2, 0, 1, 3).reshape(TOK_DEV, QHEADS * ADIM).astype(jnp.bfloat16)
    starts = jnp.arange(blocks, dtype=jnp.int32) * TOK_DEV
    result = lax.map(one_block, (query_blocks, starts))
    return result.reshape(TOKENS, QHEADS * ADIM)

def reference(mamba_input, mamba_bc, gate_input, step_input, step_bias, decay_rate, skip_gain, conv_weight, conv_bc_weight, norm_gain, queries, attn_keys, attn_values, documents):
    mixers = []
    attended_list = []
    for section_index in range(SECTIONS):
        mixers.append(mamba_section(mamba_input[section_index], mamba_bc[section_index], gate_input[section_index], step_input[section_index], step_bias[section_index], decay_rate[section_index], skip_gain[section_index], conv_weight[section_index], conv_bc_weight[section_index], norm_gain[section_index]))
        attended_list.append(attend_section(queries[section_index], attn_keys[section_index], attn_values[section_index], documents[section_index]))
    return (jnp.roll(jnp.stack(mixers), 1, axis=0), jnp.roll(jnp.stack(attended_list), 1, axis=0))
```

```python
import functools
import math

import jax
import jax.numpy as jnp
from jax import lax
from jax.experimental import pallas as pl
from jax.experimental.pallas import tpu as pltpu
from jax.sharding import PartitionSpec as P

HDIM = 64
STATE = 128
KERNEL = 4
ADIM = 128
HALO = 16
LANES = 256
ROWS = 128
MESH = pl.DeviceIdType.MESH
highest = lax.Precision.HIGHEST


def silu(v):
    return v / (1.0 + jnp.exp(-v))


def split2(v):
    high = v.astype(jnp.bfloat16)
    return high, (v - high.astype(jnp.float32)).astype(jnp.bfloat16)


def split3(v):
    high = v.astype(jnp.bfloat16)
    rest = v - high.astype(jnp.float32)
    mid = rest.astype(jnp.bfloat16)
    low = (rest - mid.astype(jnp.float32)).astype(jnp.bfloat16)
    return jnp.concatenate([high, mid, low], axis=1)


def mm(a, b):
    return jnp.dot(a, b, preferred_element_type=jnp.float32)


def nt(a, b, precision=None):
    return lax.dot_general(
        a, b, (((1,), (1,)), ((), ())), precision=precision, preferred_element_type=jnp.float32
    )


def kernel(
    n_ctx,
    n_pipe,
    x_ref,
    bc_ref,
    z_ref,
    step_ref,
    bias_ref,
    rate_ref,
    skip_ref,
    cw_ref,
    cbw_ref,
    gain_ref,
    q_ref,
    k_ref,
    v_ref,
    doc_ref,
    mix_out,
    attn_out,
    kv_scr,
    halo_x,
    halo_bc,
    state_in,
    state_out,
    attn_scr,
    mix_scr,
    doc_scr,
    mask_scr,
    expand,
    x_ext,
    bc_ext,
    xc_scr,
    xt_hi,
    xt_lo,
    g_hi,
    g_lo,
    state_acc,
    gated,
    acc_scr,
    ml_scr,
    kv_send,
    kv_recv,
    halo_send,
    halo_recv,
    st_send,
    st_recv,
    at_send,
    at_recv,
    mx_send,
    mx_recv,
):
    me = lax.axis_index("ctx")
    stage = lax.axis_index("pipe")
    following = lax.rem(stage + 1, n_pipe)
    previous = lax.rem(stage + n_pipe - 1, n_pipe)
    rows, width = x_ref.shape
    heads = q_ref.shape[1] // ADIM
    blocks = rows // ROWS

    barrier = pltpu.get_barrier_semaphore()
    pl.semaphore_signal(barrier, inc=1, device_id={"pipe": following}, device_id_type=MESH)
    pl.semaphore_signal(barrier, inc=1, device_id={"pipe": previous}, device_id_type=MESH)
    for d in range(1, n_ctx):
        pl.semaphore_signal(
            barrier, inc=1, device_id={"ctx": lax.rem(me + d, n_ctx)}, device_id_type=MESH
        )
    pl.semaphore_wait(barrier, n_ctx + 1)

    def kv_copy(d, which):
        return pltpu.make_async_remote_copy(
            src_ref=(k_ref, v_ref)[which],
            dst_ref=kv_scr.at[which, d - 1],
            send_sem=kv_send.at[which, d - 1],
            recv_sem=kv_recv.at[which, d - 1],
            device_id={"ctx": lax.rem(me + d, n_ctx)},
            device_id_type=MESH,
        )

    def halo_copy(which):
        src, dst = ((x_ref, halo_x), (bc_ref, halo_bc))[which]
        return pltpu.make_async_remote_copy(
            src_ref=src.at[rows - HALO : rows],
            dst_ref=dst,
            send_sem=halo_send.at[which],
            recv_sem=halo_recv.at[which],
            device_id={"ctx": lax.rem(me + 1, n_ctx)},
            device_id_type=MESH,
        )

    def state_copy():
        return pltpu.make_async_remote_copy(
            src_ref=state_out,
            dst_ref=state_in,
            send_sem=st_send,
            recv_sem=st_recv,
            device_id={"ctx": lax.rem(me + 1, n_ctx)},
            device_id_type=MESH,
        )

    def attn_copy(h):
        columns = pl.ds(pl.multiple_of(h * ADIM, ADIM), ADIM)
        return pltpu.make_async_remote_copy(
            src_ref=attn_scr.at[h],
            dst_ref=attn_out.at[0, :, columns],
            send_sem=at_send.at[h],
            recv_sem=at_recv.at[h],
            device_id={"pipe": following},
            device_id_type=MESH,
        )

    def mix_copy(r):
        part = pl.ds(r * ROWS, ROWS)
        return pltpu.make_async_remote_copy(
            src_ref=mix_scr.at[part],
            dst_ref=mix_out.at[0, part],
            send_sem=mx_send.at[r],
            recv_sem=mx_recv.at[r],
            device_id={"pipe": following},
            device_id_type=MESH,
        )

    for d in range(1, n_ctx):

        @pl.when(me + d < n_ctx)
        def _():
            kv_copy(d, 0).start()
            kv_copy(d, 1).start()

    for which in range(2):
        halo_copy(which).start()

    row = lax.broadcasted_iota(jnp.int32, (rows, rows), 0)
    col = lax.broadcasted_iota(jnp.int32, (rows, rows), 1)

    def doc_row(shard):
        columns = pl.ds(pl.multiple_of(shard * rows, 128), rows)
        return doc_ref[:, columns].astype(jnp.float32)

    own_docs = jnp.broadcast_to(doc_row(me), (rows, rows))
    doc_scr[...] = own_docs.T
    mask_scr[...] = jnp.where((row >= col) & (own_docs == doc_scr[...]), 0.0, -1e30)

    for d in range(1, n_ctx):

        @pl.when(me - d >= 0)
        def _():
            kv_copy(d, 0).wait_recv()
            kv_copy(d, 1).wait_recv()

    scale = 1.0 / math.sqrt(ADIM)

    def one_head(h, carry):
        columns = pl.ds(pl.multiple_of(h * ADIM, ADIM), ADIM)
        query = q_ref[:, columns]
        logits = nt(query, k_ref[...]) * scale + mask_scr[...]
        top = jnp.max(logits, axis=1, keepdims=True)
        probs = jnp.exp(logits - top)
        ml_scr[0] = top
        ml_scr[1] = jnp.sum(probs, axis=1, keepdims=True)
        acc_scr[...] = mm(probs.astype(jnp.bfloat16), v_ref[...])
        for d in range(1, n_ctx):

            @pl.when(me - d >= 0)
            def _():
                shard = lax.rem(me - d + n_ctx, n_ctx)
                logits = nt(query, kv_scr[0, d - 1]) * scale
                logits = jnp.where(doc_row(shard) == doc_scr[...], logits, -1e30)
                old = ml_scr[0]
                top = jnp.maximum(old, jnp.max(logits, axis=1, keepdims=True))
                probs = jnp.exp(logits - top)
                fade = jnp.exp(old - top)
                ml_scr[0] = top
                ml_scr[1] = ml_scr[1] * fade + jnp.sum(probs, axis=1, keepdims=True)
                acc_scr[...] = acc_scr[...] * fade + mm(
                    probs.astype(jnp.bfloat16), kv_scr[1, d - 1]
                )

        attn_scr[h] = (acc_scr[...] / ml_scr[1]).astype(jnp.bfloat16)
        attn_copy(h).start()
        return carry

    lax.fori_loop(0, heads, one_head, 0)

    count = step_ref.shape[1]
    e_row = lax.rem(lax.broadcasted_iota(jnp.int32, (3 * count, width), 0), count)
    e_col = lax.broadcasted_iota(jnp.int32, (3 * count, width), 1) // HDIM
    expand[...] = jnp.where(e_row == e_col, 1.0, 0.0).astype(jnp.bfloat16)

    for which in range(2):
        halo_copy(which).wait_recv()
    keep = jnp.where(me > 0, 1.0, 0.0)
    x_ext[0:8] = halo_x[...].astype(jnp.float32)[HALO - 8 :] * keep
    x_ext[8 : 8 + rows] = x_ref[...].astype(jnp.float32)
    bc_ext[0:8] = halo_bc[...].astype(jnp.float32)[HALO - 8 :] * keep
    bc_ext[8 : 8 + rows] = bc_ref[...].astype(jnp.float32)
    first = 8 - (KERNEL - 1)

    def bc_conv(which):
        lanes = slice(which * STATE, (which + 1) * STATE)
        total = jnp.zeros((rows, STATE), jnp.float32)
        for tap in range(KERNEL):
            total = total + cbw_ref[tap, which : which + 1] * bc_ext[first + tap : first + tap + rows, lanes]
        return silu(total)

    b_conv = bc_conv(0)
    c_conv = bc_conv(1)
    gram = jnp.where(row >= col, nt(c_conv, b_conv, highest), 0.0)
    high, low = split2(gram)
    g_hi[...] = high
    g_lo[...] = low
    bt_hi, bt_lo = split2(b_conv.T)
    c_hi, c_lo = split2(c_conv)

    raw = step_ref[...].astype(jnp.float32) + bias_ref[...]
    step = jnp.maximum(raw, 0.0) + jnp.log1p(jnp.exp(-jnp.abs(raw)))
    log_decay = -rate_ref[...] * step
    lower = jnp.where(row >= col, 1.0, 0.0)
    cumulative = jnp.dot(lower, log_decay, precision=highest, preferred_element_type=jnp.float32)
    grow = split3(jnp.exp(-cumulative) * step)
    fall = split3(jnp.exp(cumulative))
    skip = split3(jnp.broadcast_to(skip_ref[...], (8, count)))

    def prepare(j, carry):
        lanes = pl.ds(pl.multiple_of(j * LANES, LANES), LANES)
        total = cw_ref[0:1, lanes] * x_ext[first : first + rows, lanes]
        for tap in range(1, KERNEL):
            total = total + cw_ref[tap : tap + 1, lanes] * x_ext[first + tap : first + tap + rows, lanes]
        conv = silu(total)
        xc_scr[:, lanes] = conv
        high, low = split2(conv * mm(grow, expand[:, lanes]))
        xt_hi[:, lanes] = high
        xt_lo[:, lanes] = low
        state_acc[:, lanes] = mm(bt_hi, high) + mm(bt_hi, low) + mm(bt_lo, high)
        return carry

    lax.fori_loop(0, width // LANES, prepare, 0)

    @pl.when(me == 0)
    def _():
        state_in[...] = jnp.zeros_like(state_in)

    if n_ctx > 1:

        @pl.when(me > 0)
        def _():
            state_copy().wait_recv()

        @pl.when(me < n_ctx - 1)
        def _():
            end = mm(fall[rows - 16 :], expand[...])[15:16]
            state_out[...] = (end * (state_in[...].astype(jnp.float32) + state_acc[...])).astype(
                jnp.bfloat16
            )
            state_copy().start()

    for r in range(blocks):
        part = slice(r * ROWS, (r + 1) * ROWS)
        upto = (r + 1) * ROWS

        def mix_lanes(j, square):
            lanes = pl.ds(pl.multiple_of(j * LANES, LANES), LANES)
            inside = mm(g_hi[part, :upto], xt_hi[:upto, lanes])
            inside = inside + mm(g_hi[part, :upto], xt_lo[:upto, lanes])
            inside = inside + mm(g_lo[part, :upto], xt_hi[:upto, lanes])
            carried = state_in[:, lanes]
            inside = inside + mm(c_hi[part], carried) + mm(c_lo[part], carried)
            e_part = expand[:, lanes]
            out = inside * mm(fall[part], e_part) + mm(skip, e_part)[0:1] * xc_scr[part, lanes]
            out = out * silu(z_ref[part, lanes].astype(jnp.float32))
            gated[:, lanes] = out
            return square + jnp.sum(out * out, axis=1, keepdims=True)

        square = lax.fori_loop(0, width // LANES, mix_lanes, jnp.zeros((ROWS, 1), jnp.float32))
        norm = lax.rsqrt(square * (1.0 / width) + 1e-05)
        mix_scr[part] = (gated[...] * norm * gain_ref[...]).astype(jnp.bfloat16)
        mix_copy(r).start()

    for d in range(1, n_ctx):

        @pl.when(me + d < n_ctx)
        def _():
            kv_copy(d, 0).wait_send()
            kv_copy(d, 1).wait_send()

    for which in range(2):
        halo_copy(which).wait_send()
    if n_ctx > 1:

        @pl.when(me < n_ctx - 1)
        def _():
            state_copy().wait_send()

    def finish(h, carry):
        attn_copy(h).wait()
        return carry

    lax.fori_loop(0, heads, finish, 0)
    for r in range(blocks):
        mix_copy(r).wait()


def local(
    mamba_input,
    mamba_bc,
    gate_input,
    step_input,
    step_bias,
    decay_rate,
    skip_gain,
    conv_weight,
    conv_bc_weight,
    norm_gain,
    queries,
    attn_keys,
    attn_values,
    documents,
):
    n_ctx = lax.axis_size("ctx")
    n_pipe = lax.axis_size("pipe")
    _, rows, width = mamba_input.shape
    q_width = queries.shape[2]
    heads = q_width // ADIM
    count = step_input.shape[2]
    bf16, f32 = jnp.bfloat16, jnp.float32
    others = max(n_ctx - 1, 1)
    dma = pltpu.SemaphoreType.DMA
    vmem = pl.BlockSpec(memory_space=pltpu.VMEM)
    mixer, attended = pl.pallas_call(
        functools.partial(kernel, n_ctx, n_pipe),
        out_shape=(
            jax.ShapeDtypeStruct(mamba_input.shape, bf16),
            jax.ShapeDtypeStruct(queries.shape, bf16),
        ),
        in_specs=[vmem] * 14,
        out_specs=[pl.BlockSpec(memory_space=pl.ANY)] * 2,
        scratch_shapes=[
            pltpu.VMEM((2, others, rows, ADIM), bf16),
            pltpu.VMEM((HALO, width), bf16),
            pltpu.VMEM((HALO, 2 * STATE), bf16),
            pltpu.VMEM((STATE, width), bf16),
            pltpu.VMEM((STATE, width), bf16),
            pltpu.VMEM((heads, rows, ADIM), bf16),
            pltpu.VMEM((rows, width), bf16),
            pltpu.VMEM((rows, rows), f32),
            pltpu.VMEM((rows, rows), f32),
            pltpu.VMEM((3 * count, width), bf16),
            pltpu.VMEM((rows + 8, width), f32),
            pltpu.VMEM((rows + 8, 2 * STATE), f32),
            pltpu.VMEM((rows, width), f32),
            pltpu.VMEM((rows, width), bf16),
            pltpu.VMEM((rows, width), bf16),
            pltpu.VMEM((rows, rows), bf16),
            pltpu.VMEM((rows, rows), bf16),
            pltpu.VMEM((STATE, width), f32),
            pltpu.VMEM((ROWS, width), f32),
            pltpu.VMEM((rows, ADIM), f32),
            pltpu.VMEM((2, rows, 1), f32),
            dma((2, others)),
            dma((2, others)),
            dma((2,)),
            dma((2,)),
            dma,
            dma,
            dma((heads,)),
            dma((heads,)),
            dma((rows // ROWS,)),
            dma((rows // ROWS,)),
        ],
        compiler_params=pltpu.CompilerParams(
            collective_id=0, has_side_effects=True, vmem_limit_bytes=48 * 1024 * 1024
        ),
    )(
        mamba_input[0],
        mamba_bc[0].reshape(rows, 2 * STATE),
        gate_input[0],
        step_input[0],
        step_bias,
        decay_rate,
        skip_gain,
        conv_weight[0],
        conv_bc_weight[0],
        norm_gain,
        queries[0],
        attn_keys[0],
        attn_values[0],
        documents,
    )
    return mixer, attended


def solution(mesh):
    in_specs = (
        P("pipe", "ctx", "tp"),
        P("pipe", "ctx", None, "tp"),
        P("pipe", "ctx", "tp"),
        P("pipe", "ctx", "tp"),
        P("pipe", "tp"),
        P("pipe", "tp"),
        P("pipe", "tp"),
        P("pipe", None, "tp"),
        P("pipe", None, None, "tp"),
        P("pipe", "tp"),
        P("pipe", "ctx", "tp"),
        P("pipe", "ctx", "tp"),
        P("pipe", "ctx", "tp"),
        P("pipe", None),
    )
    out_specs = (P("pipe", "ctx", "tp"), P("pipe", "ctx", "tp"))
    return jax.shard_map(local, mesh=mesh, in_specs=in_specs, out_specs=out_specs, check_vma=False)
```

```python
import functools
import math

import jax
import jax.numpy as jnp
from jax import lax
from jax.experimental import pallas as pl
from jax.experimental.pallas import tpu as pltpu
from jax.sharding import PartitionSpec as P

HDIM = 64
STATE = 128
KERNEL = 4
ADIM = 128
HALO = 16
LANES = 256
ROWS = 128
MESH = pl.DeviceIdType.MESH
highest = lax.Precision.HIGHEST


def silu(v):
    return v / (1.0 + jnp.exp(-v))


def split2(v):
    high = v.astype(jnp.bfloat16)
    return high, (v - high.astype(jnp.float32)).astype(jnp.bfloat16)


def split3(v):
    high = v.astype(jnp.bfloat16)
    rest = v - high.astype(jnp.float32)
    mid = rest.astype(jnp.bfloat16)
    low = (rest - mid.astype(jnp.float32)).astype(jnp.bfloat16)
    return jnp.concatenate([high, mid, low], axis=1)


def mm(a, b):
    return jnp.dot(a, b, preferred_element_type=jnp.float32)


def nt(a, b, precision=None):
    return lax.dot_general(
        a, b, (((1,), (1,)), ((), ())), precision=precision, preferred_element_type=jnp.float32
    )


def kernel(
    n_ctx,
    n_pipe,
    x_hbm,
    bc_hbm,
    z_hbm,
    step_hbm,
    bias_hbm,
    rate_hbm,
    skip_hbm,
    cw_hbm,
    cbw_hbm,
    gain_hbm,
    q_hbm,
    k_hbm,
    v_hbm,
    doc_hbm,
    mix_out,
    attn_out,
    x_ref,
    bc_ref,
    z_ref,
    step_ref,
    bias_ref,
    rate_ref,
    skip_ref,
    cw_ref,
    cbw_ref,
    gain_ref,
    q_ref,
    k_ref,
    v_ref,
    doc_ref,
    load_sem,
    kv_scr,
    halo_x,
    halo_bc,
    state_in,
    state_out,
    attn_scr,
    mix_scr,
    doc_scr,
    mask_scr,
    expand,
    x_ext,
    bc_ext,
    xc_scr,
    xt_hi,
    xt_lo,
    g_hi,
    g_lo,
    state_acc,
    gated,
    acc_scr,
    ml_scr,
    kv_send,
    kv_recv,
    halo_send,
    halo_recv,
    st_send,
    st_recv,
    at_send,
    at_recv,
    mx_send,
    mx_recv,
):
    me = lax.axis_index("ctx")
    stage = lax.axis_index("pipe")
    following = lax.rem(stage + 1, n_pipe)
    previous = lax.rem(stage + n_pipe - 1, n_pipe)
    rows, width = x_ref.shape
    heads = q_ref.shape[1] // ADIM
    blocks = rows // ROWS

    sources = (x_hbm, bc_hbm, z_hbm, step_hbm, bias_hbm, rate_hbm, skip_hbm)
    sources += (cw_hbm, cbw_hbm, gain_hbm, q_hbm, k_hbm, v_hbm, doc_hbm)
    targets = (x_ref, bc_ref, z_ref, step_ref, bias_ref, rate_ref, skip_ref)
    targets += (cw_ref, cbw_ref, gain_ref, q_ref, k_ref, v_ref, doc_ref)
    loads = [
        pltpu.make_async_copy(source, target, load_sem.at[i])
        for i, (source, target) in enumerate(zip(sources, targets))
    ]
    for i in (13, 11, 12, 10, 0, 1, 3, 4, 5, 6, 7, 8, 9, 2):
        loads[i].start()

    barrier = pltpu.get_barrier_semaphore()
    pl.semaphore_signal(barrier, inc=1, device_id={"pipe": following}, device_id_type=MESH)
    pl.semaphore_signal(barrier, inc=1, device_id={"pipe": previous}, device_id_type=MESH)
    for d in range(1, n_ctx):
        pl.semaphore_signal(
            barrier, inc=1, device_id={"ctx": lax.rem(me + d, n_ctx)}, device_id_type=MESH
        )
    def kv_copy(d, which):
        return pltpu.make_async_remote_copy(
            src_ref=(k_hbm, v_hbm)[which],
            dst_ref=kv_scr.at[which, d - 1],
            send_sem=kv_send.at[which, d - 1],
            recv_sem=kv_recv.at[which, d - 1],
            device_id={"ctx": lax.rem(me + d, n_ctx)},
            device_id_type=MESH,
        )

    def halo_copy(which):
        src, dst = ((x_hbm, halo_x), (bc_hbm, halo_bc))[which]
        return pltpu.make_async_remote_copy(
            src_ref=src.at[src.shape[0] - dst.shape[0] : src.shape[0]],
            dst_ref=dst,
            send_sem=halo_send.at[which],
            recv_sem=halo_recv.at[which],
            device_id={"ctx": lax.rem(me + 1, n_ctx)},
            device_id_type=MESH,
        )

    def state_copy():
        return pltpu.make_async_remote_copy(
            src_ref=state_out,
            dst_ref=state_in,
            send_sem=st_send,
            recv_sem=st_recv,
            device_id={"ctx": lax.rem(me + 1, n_ctx)},
            device_id_type=MESH,
        )

    def attn_copy(h):
        columns = pl.ds(pl.multiple_of(h * ADIM, ADIM), ADIM)
        return pltpu.make_async_remote_copy(
            src_ref=attn_scr.at[h],
            dst_ref=attn_out.at[0, :, columns],
            send_sem=at_send.at[h],
            recv_sem=at_recv.at[h],
            device_id={"pipe": following},
            device_id_type=MESH,
        )

    def mix_copy(r):
        part = pl.ds(r * ROWS, ROWS)
        return pltpu.make_async_remote_copy(
            src_ref=mix_scr.at[part],
            dst_ref=mix_out.at[0, part],
            send_sem=mx_send.at[r],
            recv_sem=mx_recv.at[r],
            device_id={"pipe": following},
            device_id_type=MESH,
        )

    row = lax.broadcasted_iota(jnp.int32, (rows, rows), 0)
    col = lax.broadcasted_iota(jnp.int32, (rows, rows), 1)

    def doc_row(shard):
        columns = pl.ds(pl.multiple_of(shard * rows, 128), rows)
        return doc_ref[:, columns].astype(jnp.float32)

    pl.semaphore_wait(barrier, n_ctx + 1)

    for d in range(1, n_ctx):

        @pl.when(me + d < n_ctx)
        def _():
            kv_copy(d, 0).start()
            kv_copy(d, 1).start()

    for which in range(2):
        halo_copy(which).start()

    loads[13].wait()
    own_docs = jnp.broadcast_to(doc_row(me), (rows, rows))
    doc_scr[...] = own_docs.T
    mask_scr[...] = jnp.where((row >= col) & (own_docs == doc_scr[...]), 0.0, -1e30)

    for i in (11, 12, 10):
        loads[i].wait()

    for d in range(1, n_ctx):

        @pl.when(me - d >= 0)
        def _():
            kv_copy(d, 0).wait_recv()
            kv_copy(d, 1).wait_recv()

    scale = 1.0 / math.sqrt(ADIM)

    def one_head(h, carry):
        columns = pl.ds(pl.multiple_of(h * ADIM, ADIM), ADIM)
        query = q_ref[:, columns]
        logits = nt(query, k_ref[...]) * scale + mask_scr[...]
        top = jnp.max(logits, axis=1, keepdims=True)
        probs = jnp.exp(logits - top)
        ml_scr[0] = top
        ml_scr[1] = jnp.sum(probs, axis=1, keepdims=True)
        acc_scr[...] = mm(probs.astype(jnp.bfloat16), v_ref[...])
        for d in range(1, n_ctx):

            @pl.when(me - d >= 0)
            def _():
                shard = lax.rem(me - d + n_ctx, n_ctx)
                logits = nt(query, kv_scr[0, d - 1]) * scale
                logits = jnp.where(doc_row(shard) == doc_scr[...], logits, -1e30)
                old = ml_scr[0]
                top = jnp.maximum(old, jnp.max(logits, axis=1, keepdims=True))
                probs = jnp.exp(logits - top)
                fade = jnp.exp(old - top)
                ml_scr[0] = top
                ml_scr[1] = ml_scr[1] * fade + jnp.sum(probs, axis=1, keepdims=True)
                acc_scr[...] = acc_scr[...] * fade + mm(
                    probs.astype(jnp.bfloat16), kv_scr[1, d - 1]
                )

        attn_scr[h] = (acc_scr[...] / ml_scr[1]).astype(jnp.bfloat16)
        attn_copy(h).start()
        return carry

    lax.fori_loop(0, heads, one_head, 0)

    count = step_ref.shape[0]
    e_row = lax.rem(lax.broadcasted_iota(jnp.int32, (3 * count, width), 0), count)
    e_col = lax.broadcasted_iota(jnp.int32, (3 * count, width), 1) // HDIM
    expand[...] = jnp.where(e_row == e_col, 1.0, 0.0).astype(jnp.bfloat16)

    for i in (0, 1, 3, 4, 5, 6, 7, 8):
        loads[i].wait()
    for which in range(2):
        halo_copy(which).wait_recv()
    keep = jnp.where(me > 0, 1.0, 0.0)
    x_ext[0:8] = halo_x[...].astype(jnp.float32)[HALO - 8 :] * keep
    x_ext[8 : 8 + rows] = x_ref[...].astype(jnp.float32)
    bc_ext[0:16] = halo_bc[...].astype(jnp.float32)[2 * HALO - 16 :] * keep
    bc_ext[16 : 16 + 2 * rows] = bc_ref[...].astype(jnp.float32)
    first = 8 - (KERNEL - 1)

    def bc_conv(which):
        total = jnp.zeros((rows, STATE), jnp.float32)
        for tap in range(KERNEL):
            tokens = bc_ext[pl.ds(2 * (first + tap) + which, rows, stride=2)]
            total = total + cbw_ref[tap, which : which + 1] * tokens
        return silu(total)

    b_conv = bc_conv(0)
    c_conv = bc_conv(1)
    gram = jnp.where(row >= col, nt(c_conv, b_conv, highest), 0.0)
    high, low = split2(gram)
    g_hi[...] = high
    g_lo[...] = low
    bt_hi, bt_lo = split2(b_conv.T)
    c_hi, c_lo = split2(c_conv)

    raw = step_ref[...].astype(jnp.float32).T + bias_ref[...]
    step = jnp.maximum(raw, 0.0) + jnp.log1p(jnp.exp(-jnp.abs(raw)))
    log_decay = -rate_ref[...] * step
    lower = jnp.where(row >= col, 1.0, 0.0)
    cumulative = jnp.dot(lower, log_decay, precision=highest, preferred_element_type=jnp.float32)
    grow = split3(jnp.exp(-cumulative) * step)
    fall = split3(jnp.exp(cumulative))
    skip = split3(jnp.broadcast_to(skip_ref[...], (8, count)))

    def prepare(j, carry):
        lanes = pl.ds(pl.multiple_of(j * LANES, LANES), LANES)
        total = cw_ref[0:1, lanes] * x_ext[first : first + rows, lanes]
        for tap in range(1, KERNEL):
            total = total + cw_ref[tap : tap + 1, lanes] * x_ext[first + tap : first + tap + rows, lanes]
        conv = silu(total)
        xc_scr[:, lanes] = conv
        high, low = split2(conv * mm(grow, expand[:, lanes]))
        xt_hi[:, lanes] = high
        xt_lo[:, lanes] = low
        state_acc[:, lanes] = mm(bt_hi, high) + mm(bt_hi, low) + mm(bt_lo, high)
        return carry

    lax.fori_loop(0, width // LANES, prepare, 0)

    @pl.when(me == 0)
    def _():
        state_in[...] = jnp.zeros_like(state_in)

    if n_ctx > 1:

        @pl.when(me > 0)
        def _():
            state_copy().wait_recv()

        @pl.when(me < n_ctx - 1)
        def _():
            end = mm(fall[rows - 16 :], expand[...])[15:16]
            state_out[...] = (end * (state_in[...].astype(jnp.float32) + state_acc[...])).astype(
                jnp.bfloat16
            )
            state_copy().start()

    loads[2].wait()
    loads[9].wait()
    for r in range(blocks):
        part = slice(r * ROWS, (r + 1) * ROWS)
        upto = (r + 1) * ROWS

        def mix_lanes(j, square):
            lanes = pl.ds(pl.multiple_of(j * LANES, LANES), LANES)
            inside = mm(g_hi[part, :upto], xt_hi[:upto, lanes])
            inside = inside + mm(g_hi[part, :upto], xt_lo[:upto, lanes])
            inside = inside + mm(g_lo[part, :upto], xt_hi[:upto, lanes])
            carried = state_in[:, lanes]
            inside = inside + mm(c_hi[part], carried) + mm(c_lo[part], carried)
            e_part = expand[:, lanes]
            out = inside * mm(fall[part], e_part) + mm(skip, e_part)[0:1] * xc_scr[part, lanes]
            out = out * silu(z_ref[part, lanes].astype(jnp.float32))
            gated[:, lanes] = out
            return square + jnp.sum(out * out, axis=1, keepdims=True)

        square = lax.fori_loop(0, width // LANES, mix_lanes, jnp.zeros((ROWS, 1), jnp.float32))
        norm = lax.rsqrt(square * (1.0 / width) + 1e-05)
        mix_scr[part] = (gated[...] * norm * gain_ref[...]).astype(jnp.bfloat16)
        mix_copy(r).start()

    for d in range(1, n_ctx):

        @pl.when(me + d < n_ctx)
        def _():
            kv_copy(d, 0).wait_send()
            kv_copy(d, 1).wait_send()

    for which in range(2):
        halo_copy(which).wait_send()
    if n_ctx > 1:

        @pl.when(me < n_ctx - 1)
        def _():
            state_copy().wait_send()

    def finish(h, carry):
        attn_copy(h).wait()
        return carry

    lax.fori_loop(0, heads, finish, 0)
    for r in range(blocks):
        mix_copy(r).wait()


def local(
    mamba_input,
    mamba_bc,
    gate_input,
    step_input,
    step_bias,
    decay_rate,
    skip_gain,
    conv_weight,
    conv_bc_weight,
    norm_gain,
    queries,
    attn_keys,
    attn_values,
    documents,
):
    n_ctx = lax.axis_size("ctx")
    n_pipe = lax.axis_size("pipe")
    _, rows, width = mamba_input.shape
    q_width = queries.shape[2]
    heads = q_width // ADIM
    count = step_input.shape[2]
    bf16, f32 = jnp.bfloat16, jnp.float32
    others = max(n_ctx - 1, 1)
    dma = pltpu.SemaphoreType.DMA
    operands = (
        mamba_input[0],
        mamba_bc[0].reshape(2 * rows, STATE),
        gate_input[0],
        step_input[0].T,
        step_bias,
        decay_rate,
        skip_gain,
        conv_weight[0],
        conv_bc_weight[0],
        norm_gain,
        queries[0],
        attn_keys[0],
        attn_values[0],
        documents,
    )
    mixer, attended = pl.pallas_call(
        functools.partial(kernel, n_ctx, n_pipe),
        out_shape=(
            jax.ShapeDtypeStruct(mamba_input.shape, bf16),
            jax.ShapeDtypeStruct(queries.shape, bf16),
        ),
        in_specs=[pl.BlockSpec(memory_space=pltpu.HBM)] * len(operands),
        out_specs=[pl.BlockSpec(memory_space=pl.ANY)] * 2,
        scratch_shapes=[pltpu.VMEM(operand.shape, operand.dtype) for operand in operands]
        + [
            dma((len(operands),)),
            pltpu.VMEM((2, others, rows, ADIM), bf16),
            pltpu.VMEM((HALO, width), bf16),
            pltpu.VMEM((2 * HALO, STATE), bf16),
            pltpu.VMEM((STATE, width), bf16),
            pltpu.VMEM((STATE, width), bf16),
            pltpu.VMEM((heads, rows, ADIM), bf16),
            pltpu.VMEM((rows, width), bf16),
            pltpu.VMEM((rows, rows), f32),
            pltpu.VMEM((rows, rows), f32),
            pltpu.VMEM((3 * count, width), bf16),
            pltpu.VMEM((rows + 8, width), f32),
            pltpu.VMEM((2 * rows + 16, STATE), f32),
            pltpu.VMEM((rows, width), f32),
            pltpu.VMEM((rows, width), bf16),
            pltpu.VMEM((rows, width), bf16),
            pltpu.VMEM((rows, rows), bf16),
            pltpu.VMEM((rows, rows), bf16),
            pltpu.VMEM((STATE, width), f32),
            pltpu.VMEM((ROWS, width), f32),
            pltpu.VMEM((rows, ADIM), f32),
            pltpu.VMEM((2, rows, 1), f32),
            dma((2, others)),
            dma((2, others)),
            dma((2,)),
            dma((2,)),
            dma,
            dma,
            dma((heads,)),
            dma((heads,)),
            dma((rows // ROWS,)),
            dma((rows // ROWS,)),
        ],
        compiler_params=pltpu.CompilerParams(
            collective_id=0, has_side_effects=True, vmem_limit_bytes=62_000_000
        ),
    )(*operands)
    return mixer, attended


def solution(mesh):
    in_specs = (
        P("pipe", "ctx", "tp"),
        P("pipe", "ctx", None, "tp"),
        P("pipe", "ctx", "tp"),
        P("pipe", "ctx", "tp"),
        P("pipe", "tp"),
        P("pipe", "tp"),
        P("pipe", "tp"),
        P("pipe", None, "tp"),
        P("pipe", None, None, "tp"),
        P("pipe", "tp"),
        P("pipe", "ctx", "tp"),
        P("pipe", "ctx", "tp"),
        P("pipe", "ctx", "tp"),
        P("pipe", None),
    )
    out_specs = (P("pipe", "ctx", "tp"), P("pipe", "ctx", "tp"))
    return jax.shard_map(local, mesh=mesh, in_specs=in_specs, out_specs=out_specs, check_vma=False)
```

```python
import functools
import math

import jax
import jax.numpy as jnp
from jax import lax
from jax.experimental import pallas as pl
from jax.experimental.pallas import tpu as pltpu
from jax.sharding import PartitionSpec as P

HDIM = 64
STATE = 128
KERNEL = 4
ADIM = 128
HALO = 16
LANES = 256
ROWS = 128
MESH = pl.DeviceIdType.MESH
highest = lax.Precision.HIGHEST


def silu(v):
    return v / (1.0 + jnp.exp(-v))


def split2(v):
    high = v.astype(jnp.bfloat16)
    return high, (v - high.astype(jnp.float32)).astype(jnp.bfloat16)


def split3(v):
    high = v.astype(jnp.bfloat16)
    rest = v - high.astype(jnp.float32)
    mid = rest.astype(jnp.bfloat16)
    low = (rest - mid.astype(jnp.float32)).astype(jnp.bfloat16)
    return jnp.concatenate([high, mid, low], axis=1)


def mm(a, b):
    return jnp.dot(a, b, preferred_element_type=jnp.float32)


def nt(a, b, precision=None):
    return lax.dot_general(
        a, b, (((1,), (1,)), ((), ())), precision=precision, preferred_element_type=jnp.float32
    )


def kernel(
    n_ctx,
    n_pipe,
    x_hbm,
    bc_hbm,
    z_hbm,
    step_hbm,
    bias_hbm,
    rate_hbm,
    skip_hbm,
    cw_hbm,
    cbw_hbm,
    gain_hbm,
    q_hbm,
    k_hbm,
    v_hbm,
    doc_hbm,
    mix_out,
    attn_out,
    x_ref,
    bc_ref,
    z_ref,
    step_ref,
    bias_ref,
    rate_ref,
    skip_ref,
    cw_ref,
    cbw_ref,
    gain_ref,
    q_ref,
    k_ref,
    v_ref,
    doc_ref,
    load_sem,
    kv_scr,
    halo_x,
    halo_bc,
    state_in,
    state_out,
    attn_scr,
    mix_scr,
    doc_scr,
    mask_scr,
    expand,
    x_ext,
    bc_ext,
    xc_scr,
    xt_hi,
    xt_lo,
    g_hi,
    g_lo,
    state_acc,
    gated,
    acc_scr,
    ml_scr,
    kv_send,
    kv_recv,
    halo_send,
    halo_recv,
    st_send,
    st_recv,
    at_send,
    at_recv,
    mx_send,
    mx_recv,
):
    me = lax.axis_index("ctx")
    stage = lax.axis_index("pipe")
    following = lax.rem(stage + 1, n_pipe)
    previous = lax.rem(stage + n_pipe - 1, n_pipe)
    rows, width = x_ref.shape
    heads = q_ref.shape[1] // ADIM
    blocks = rows // ROWS

    sources = (x_hbm, bc_hbm, z_hbm, step_hbm, bias_hbm, rate_hbm, skip_hbm)
    sources += (cw_hbm, cbw_hbm, gain_hbm, q_hbm, k_hbm, v_hbm, doc_hbm)
    targets = (x_ref, bc_ref, z_ref, step_ref, bias_ref, rate_ref, skip_ref)
    targets += (cw_ref, cbw_ref, gain_ref, q_ref, k_ref, v_ref, doc_ref)
    loads = [
        pltpu.make_async_copy(source, target, load_sem.at[i])
        for i, (source, target) in enumerate(zip(sources, targets))
    ]
    for i in (13, 11, 12, 10, 0, 1, 3, 4, 5, 6, 7, 8, 9, 2):
        loads[i].start()

    barrier = pltpu.get_barrier_semaphore()
    pl.semaphore_signal(barrier, inc=1, device_id={"pipe": following}, device_id_type=MESH)
    pl.semaphore_signal(barrier, inc=1, device_id={"pipe": previous}, device_id_type=MESH)
    for d in range(1, n_ctx):
        pl.semaphore_signal(
            barrier, inc=1, device_id={"ctx": lax.rem(me + d, n_ctx)}, device_id_type=MESH
        )
    def kv_copy(d, which):
        return pltpu.make_async_remote_copy(
            src_ref=(k_hbm, v_hbm)[which],
            dst_ref=kv_scr.at[which, d - 1],
            send_sem=kv_send.at[which, d - 1],
            recv_sem=kv_recv.at[which, d - 1],
            device_id={"ctx": lax.rem(me + d, n_ctx)},
            device_id_type=MESH,
        )

    def halo_copy(which):
        src, dst = ((x_hbm, halo_x), (bc_hbm, halo_bc))[which]
        return pltpu.make_async_remote_copy(
            src_ref=src.at[src.shape[0] - dst.shape[0] : src.shape[0]],
            dst_ref=dst,
            send_sem=halo_send.at[which],
            recv_sem=halo_recv.at[which],
            device_id={"ctx": lax.rem(me + 1, n_ctx)},
            device_id_type=MESH,
        )

    def state_copy():
        return pltpu.make_async_remote_copy(
            src_ref=state_out,
            dst_ref=state_in,
            send_sem=st_send,
            recv_sem=st_recv,
            device_id={"ctx": lax.rem(me + 1, n_ctx)},
            device_id_type=MESH,
        )

    def attn_copy(h):
        columns = pl.ds(pl.multiple_of(h * ADIM, ADIM), ADIM)
        return pltpu.make_async_remote_copy(
            src_ref=attn_scr.at[h],
            dst_ref=attn_out.at[0, :, columns],
            send_sem=at_send.at[h],
            recv_sem=at_recv.at[h],
            device_id={"pipe": following},
            device_id_type=MESH,
        )

    def mix_copy(r):
        part = pl.ds(r * ROWS, ROWS)
        return pltpu.make_async_remote_copy(
            src_ref=mix_scr.at[part],
            dst_ref=mix_out.at[0, part],
            send_sem=mx_send.at[r],
            recv_sem=mx_recv.at[r],
            device_id={"pipe": following},
            device_id_type=MESH,
        )

    row = lax.broadcasted_iota(jnp.int32, (rows, rows), 0)
    col = lax.broadcasted_iota(jnp.int32, (rows, rows), 1)

    def doc_row(shard):
        columns = pl.ds(pl.multiple_of(shard * rows, 128), rows)
        return doc_ref[:, columns].astype(jnp.float32)

    loads[13].wait()
    own_docs = jnp.broadcast_to(doc_row(me), (rows, rows))
    doc_scr[...] = own_docs.T
    mask_scr[...] = jnp.where((row >= col) & (own_docs == doc_scr[...]), 0.0, -1e30)

    pl.semaphore_wait(barrier, n_ctx + 1)

    for d in range(1, n_ctx):

        @pl.when(me + d < n_ctx)
        def _():
            kv_copy(d, 0).start()
            kv_copy(d, 1).start()

    for which in range(2):
        halo_copy(which).start()

    for i in (11, 12, 10):
        loads[i].wait()

    for d in range(1, n_ctx):

        @pl.when(me - d >= 0)
        def _():
            kv_copy(d, 0).wait_recv()
            kv_copy(d, 1).wait_recv()

    scale = 1.0 / math.sqrt(ADIM)

    def one_head(h, carry):
        columns = pl.ds(pl.multiple_of(h * ADIM, ADIM), ADIM)
        query = q_ref[:, columns]
        logits = nt(query, k_ref[...]) * scale + mask_scr[...]
        top = jnp.max(logits, axis=1, keepdims=True)
        probs = jnp.exp(logits - top)
        ml_scr[0] = top
        ml_scr[1] = jnp.sum(probs, axis=1, keepdims=True)
        acc_scr[...] = mm(probs.astype(jnp.bfloat16), v_ref[...])
        for d in range(1, n_ctx):

            @pl.when(me - d >= 0)
            def _():
                shard = lax.rem(me - d + n_ctx, n_ctx)
                logits = nt(query, kv_scr[0, d - 1]) * scale
                logits = jnp.where(doc_row(shard) == doc_scr[...], logits, -1e30)
                old = ml_scr[0]
                top = jnp.maximum(old, jnp.max(logits, axis=1, keepdims=True))
                probs = jnp.exp(logits - top)
                fade = jnp.exp(old - top)
                ml_scr[0] = top
                ml_scr[1] = ml_scr[1] * fade + jnp.sum(probs, axis=1, keepdims=True)
                acc_scr[...] = acc_scr[...] * fade + mm(
                    probs.astype(jnp.bfloat16), kv_scr[1, d - 1]
                )

        attn_scr[h] = (acc_scr[...] / ml_scr[1]).astype(jnp.bfloat16)
        attn_copy(h).start()
        return carry

    lax.fori_loop(0, heads, one_head, 0)

    count = step_ref.shape[0]
    e_row = lax.rem(lax.broadcasted_iota(jnp.int32, (3 * count, width), 0), count)
    e_col = lax.broadcasted_iota(jnp.int32, (3 * count, width), 1) // HDIM
    expand[...] = jnp.where(e_row == e_col, 1.0, 0.0).astype(jnp.bfloat16)

    for i in (0, 1, 3, 4, 5, 6, 7, 8):
        loads[i].wait()
    for which in range(2):
        halo_copy(which).wait_recv()
    keep = jnp.where(me > 0, 1.0, 0.0)
    x_ext[0:8] = halo_x[...].astype(jnp.float32)[HALO - 8 :] * keep
    x_ext[8 : 8 + rows] = x_ref[...].astype(jnp.float32)
    bc_ext[0:16] = halo_bc[...].astype(jnp.float32)[2 * HALO - 16 :] * keep
    bc_ext[16 : 16 + 2 * rows] = bc_ref[...].astype(jnp.float32)
    first = 8 - (KERNEL - 1)

    def bc_conv(which):
        total = jnp.zeros((rows, STATE), jnp.float32)
        for tap in range(KERNEL):
            tokens = bc_ext[pl.ds(2 * (first + tap) + which, rows, stride=2)]
            total = total + cbw_ref[tap, which : which + 1] * tokens
        return silu(total)

    b_conv = bc_conv(0)
    c_conv = bc_conv(1)
    gram = jnp.where(row >= col, nt(c_conv, b_conv, highest), 0.0)
    high, low = split2(gram)
    g_hi[...] = high
    g_lo[...] = low
    bt_hi, bt_lo = split2(b_conv.T)
    c_hi, c_lo = split2(c_conv)

    raw = step_ref[...].astype(jnp.float32).T + bias_ref[...]
    step = jnp.maximum(raw, 0.0) + jnp.log1p(jnp.exp(-jnp.abs(raw)))
    log_decay = -rate_ref[...] * step
    lower = jnp.where(row >= col, 1.0, 0.0)
    cumulative = jnp.dot(lower, log_decay, precision=highest, preferred_element_type=jnp.float32)
    grow = split3(jnp.exp(-cumulative) * step)
    fall = split3(jnp.exp(cumulative))
    skip = split3(jnp.broadcast_to(skip_ref[...], (8, count)))

    def prepare(j, carry):
        lanes = pl.ds(pl.multiple_of(j * LANES, LANES), LANES)
        total = cw_ref[0:1, lanes] * x_ext[first : first + rows, lanes]
        for tap in range(1, KERNEL):
            total = total + cw_ref[tap : tap + 1, lanes] * x_ext[first + tap : first + tap + rows, lanes]
        conv = silu(total)
        xc_scr[:, lanes] = conv
        high, low = split2(conv * mm(grow, expand[:, lanes]))
        xt_hi[:, lanes] = high
        xt_lo[:, lanes] = low
        state_acc[:, lanes] = mm(bt_hi, high) + mm(bt_hi, low) + mm(bt_lo, high)
        return carry

    lax.fori_loop(0, width // LANES, prepare, 0)

    @pl.when(me == 0)
    def _():
        state_in[...] = jnp.zeros_like(state_in)

    if n_ctx > 1:

        @pl.when(me > 0)
        def _():
            state_copy().wait_recv()

        @pl.when(me < n_ctx - 1)
        def _():
            end = mm(fall[rows - 16 :], expand[...])[15:16]
            state_out[...] = (end * (state_in[...].astype(jnp.float32) + state_acc[...])).astype(
                jnp.bfloat16
            )
            state_copy().start()

    loads[2].wait()
    loads[9].wait()
    for r in range(blocks):
        part = slice(r * ROWS, (r + 1) * ROWS)
        upto = (r + 1) * ROWS

        def mix_lanes(j, square):
            lanes = pl.ds(pl.multiple_of(j * LANES, LANES), LANES)
            inside = mm(g_hi[part, :upto], xt_hi[:upto, lanes])
            inside = inside + mm(g_hi[part, :upto], xt_lo[:upto, lanes])
            inside = inside + mm(g_lo[part, :upto], xt_hi[:upto, lanes])
            carried = state_in[:, lanes]
            inside = inside + mm(c_hi[part], carried) + mm(c_lo[part], carried)
            e_part = expand[:, lanes]
            out = inside * mm(fall[part], e_part) + mm(skip, e_part)[0:1] * xc_scr[part, lanes]
            out = out * silu(z_ref[part, lanes].astype(jnp.float32))
            gated[:, lanes] = out
            return square + jnp.sum(out * out, axis=1, keepdims=True)

        square = lax.fori_loop(0, width // LANES, mix_lanes, jnp.zeros((ROWS, 1), jnp.float32))
        norm = lax.rsqrt(square * (1.0 / width) + 1e-05)
        mix_scr[part] = (gated[...] * norm * gain_ref[...]).astype(jnp.bfloat16)
        mix_copy(r).start()

    for d in range(1, n_ctx):

        @pl.when(me + d < n_ctx)
        def _():
            kv_copy(d, 0).wait_send()
            kv_copy(d, 1).wait_send()

    for which in range(2):
        halo_copy(which).wait_send()
    if n_ctx > 1:

        @pl.when(me < n_ctx - 1)
        def _():
            state_copy().wait_send()

    def finish(h, carry):
        attn_copy(h).wait()
        return carry

    lax.fori_loop(0, heads, finish, 0)
    for r in range(blocks):
        mix_copy(r).wait()


def store(mix_ref, attn_ref, mix_out, attn_out, mix_scr, attn_scr, load_sem, store_sem):
    pieces = []
    for source, stage, target in ((mix_ref, mix_scr, mix_out), (attn_ref, attn_scr, attn_out)):
        for r in range(source.shape[1] // ROWS):
            part = pl.ds(r * ROWS, ROWS)
            pieces.append((source.at[:, part], stage.at[:, part], target.at[:, part]))
    loads = [
        pltpu.make_async_copy(source, stage, load_sem.at[i])
        for i, (source, stage, _) in enumerate(pieces)
    ]
    stores = [
        pltpu.make_async_copy(stage, target, store_sem.at[i])
        for i, (_, stage, target) in enumerate(pieces)
    ]
    for load in loads:
        load.start()
    for load, put in zip(loads, stores):
        load.wait()
        put.start()
    for put in stores:
        put.wait()


def local(
    mamba_input,
    mamba_bc,
    gate_input,
    step_input,
    step_bias,
    decay_rate,
    skip_gain,
    conv_weight,
    conv_bc_weight,
    norm_gain,
    queries,
    attn_keys,
    attn_values,
    documents,
):
    n_ctx = lax.axis_size("ctx")
    n_pipe = lax.axis_size("pipe")
    _, rows, width = mamba_input.shape
    q_width = queries.shape[2]
    heads = q_width // ADIM
    count = step_input.shape[2]
    bf16, f32 = jnp.bfloat16, jnp.float32
    others = max(n_ctx - 1, 1)
    dma = pltpu.SemaphoreType.DMA
    operands = (
        mamba_input[0],
        mamba_bc[0].reshape(2 * rows, STATE),
        gate_input[0],
        step_input[0].T,
        step_bias,
        decay_rate,
        skip_gain,
        conv_weight[0],
        conv_bc_weight[0],
        norm_gain,
        queries[0],
        attn_keys[0],
        attn_values[0],
        documents,
    )
    mixer, attended = pl.pallas_call(
        functools.partial(kernel, n_ctx, n_pipe),
        out_shape=(
            jax.ShapeDtypeStruct(mamba_input.shape, bf16),
            jax.ShapeDtypeStruct(queries.shape, bf16),
        ),
        in_specs=[pl.BlockSpec(memory_space=pltpu.HBM)] * len(operands),
        out_specs=[pl.BlockSpec(memory_space=pl.ANY)] * 2,
        scratch_shapes=[pltpu.VMEM(operand.shape, operand.dtype) for operand in operands]
        + [
            dma((len(operands),)),
            pltpu.VMEM((2, others, rows, ADIM), bf16),
            pltpu.VMEM((HALO, width), bf16),
            pltpu.VMEM((2 * HALO, STATE), bf16),
            pltpu.VMEM((STATE, width), bf16),
            pltpu.VMEM((STATE, width), bf16),
            pltpu.VMEM((heads, rows, ADIM), bf16),
            pltpu.VMEM((rows, width), bf16),
            pltpu.VMEM((rows, rows), f32),
            pltpu.VMEM((rows, rows), f32),
            pltpu.VMEM((3 * count, width), bf16),
            pltpu.VMEM((rows + 8, width), f32),
            pltpu.VMEM((2 * rows + 16, STATE), f32),
            pltpu.VMEM((rows, width), f32),
            pltpu.VMEM((rows, width), bf16),
            pltpu.VMEM((rows, width), bf16),
            pltpu.VMEM((rows, rows), bf16),
            pltpu.VMEM((rows, rows), bf16),
            pltpu.VMEM((STATE, width), f32),
            pltpu.VMEM((ROWS, width), f32),
            pltpu.VMEM((rows, ADIM), f32),
            pltpu.VMEM((2, rows, 1), f32),
            dma((2, others)),
            dma((2, others)),
            dma((2,)),
            dma((2,)),
            dma,
            dma,
            dma((heads,)),
            dma((heads,)),
            dma((rows // ROWS,)),
            dma((rows // ROWS,)),
        ],
        compiler_params=pltpu.CompilerParams(
            collective_id=0, has_side_effects=True, vmem_limit_bytes=62_000_000
        ),
    )(*operands)
    return pl.pallas_call(
        store,
        out_shape=(
            jax.ShapeDtypeStruct(mamba_input.shape, bf16),
            jax.ShapeDtypeStruct(queries.shape, bf16),
        ),
        in_specs=[pl.BlockSpec(memory_space=pl.ANY)] * 2,
        out_specs=[pl.BlockSpec(memory_space=pl.ANY)] * 2,
        scratch_shapes=[
            pltpu.VMEM(mamba_input.shape, bf16),
            pltpu.VMEM(queries.shape, bf16),
            dma((2 * (rows // ROWS),)),
            dma((2 * (rows // ROWS),)),
        ],
        compiler_params=pltpu.CompilerParams(vmem_limit_bytes=62_000_000),
    )(mixer, attended)


def solution(mesh):
    in_specs = (
        P("pipe", "ctx", "tp"),
        P("pipe", "ctx", None, "tp"),
        P("pipe", "ctx", "tp"),
        P("pipe", "ctx", "tp"),
        P("pipe", "tp"),
        P("pipe", "tp"),
        P("pipe", "tp"),
        P("pipe", None, "tp"),
        P("pipe", None, None, "tp"),
        P("pipe", "tp"),
        P("pipe", "ctx", "tp"),
        P("pipe", "ctx", "tp"),
        P("pipe", "ctx", "tp"),
        P("pipe", None),
    )
    out_specs = (P("pipe", "ctx", "tp"), P("pipe", "ctx", "tp"))
    return jax.shard_map(local, mesh=mesh, in_specs=in_specs, out_specs=out_specs, check_vma=False)
```
